512 devices in a mesh: atom: 32 (over x, y_lo, core), chan: 8 (over z), rep: 2 (over y_hi).
Axes of the slice: x: 4, y: 8 (y_hi: 2, y_lo: 4; y = y_hi * 4 + y_lo), z: 8, core: 2. Of those that a mesh axis runs over, the one named last changes fastest.
Arguments:
- feats: bfloat16 [2, 128, 81, 512], P('rep', 'chan', None, 'atom'), may hold values from -6 to 6
- neighbors: int32 [2, 512, 32], P('rep', 'atom'), may hold values from 0 to 511, as said below
- counts: int32 [2, 512], P('rep', 'atom'), may hold values from 1 to 32, as said below
- radial: bfloat16 [2, 8, 16384], P('rep', None, 'atom'), may hold values from 2 to 6
- filter_weight: bfloat16 [8, 128, 81], P(None, 'chan'), may hold values from -0.3125 to 0.3125
- message_grad: bfloat16 [2, 128, 81, 16384], P('rep', 'chan', None, 'atom'), may hold values from -2 to 2
Outputs:
- feat_grad: float32 [2, 128, 81, 512], P('rep', 'chan', None, 'atom')
- radial_grad: float32 [2, 8, 16384], P('rep', None, 'atom')
- weight_grad: float32 [8, 128, 81], P(None, 'chan')
The draws below stay inside these ranges and needn't reach their ends.
Inputs may be any that keep to these rules, and one draw needn't show every extreme that they name: `neighbors`: each source atom lies, counted cyclically, in the block of 16 consecutive atoms that holds its receiver or in one of the 2 such blocks on either side. `counts`: some atom of every crystal has all 32 slots valid.
All inputs are finite; a program needn't handle non-finite values.
Results may differ from the reference program's by a relative error of at most 0.0054.
Values may be sent and summed in bfloat16 or wider, within the bound.
No kernel may reach another device: no remote copies, remote signals or barrier semaphores. Data moves between devices by JAX's collectives and lax.ppermute only.
A program may use at most 64 MiB of HBM per device.

```python
import jax
import jax.numpy as jnp
from jax import lax

C = 128
BASIS = 9
POINTS = 16
K = 8
SLOTS = 32
REACH = 2
ATOM_DEV = 16
G = 81
SAMPLES = 256
ATOMS = 512
EDGES = 16384
BATCH = 2


def draw_neighbors(key, part):
    first_key, second_key = jax.random.split(jax.random.fold_in(key, 11))
    shape = (BATCH, ATOMS, SLOTS)
    offsets = jax.random.randint(first_key, shape, -REACH, REACH + 1)
    inside = jax.random.randint(second_key, shape, 0, ATOM_DEV)
    block_count = ATOMS // ATOM_DEV
    blocks = (jnp.arange(ATOMS, dtype=jnp.int32) // ATOM_DEV)[None, :, None]
    return ((blocks + offsets) % block_count * ATOM_DEV + inside).astype(jnp.int32)


def draw_counts(key, part):
    first_key, second_key, third_key = jax.random.split(jax.random.fold_in(key, 23), 3)
    block_count = ATOMS // ATOM_DEV
    base = jax.random.randint(first_key, (BATCH, block_count), 4, SLOTS + 1)
    jitter = jax.random.randint(second_key, (BATCH, ATOMS), -3, 4)
    counted = jnp.clip(jnp.repeat(base, ATOM_DEV, axis=1) + jitter, 1, SLOTS)
    chosen = jax.random.randint(third_key, (BATCH, 1), 0, ATOMS)
    counted = jnp.where(jnp.arange(ATOMS, dtype=jnp.int32)[None, :] == chosen, SLOTS, counted)
    return counted.astype(jnp.int32)


def block_levels(rng, dims, cuts, smallest, top_value):
    loudness = 1.0
    for position, blocks in cuts:
        steps = jax.random.uniform(jax.random.fold_in(jax.random.fold_in(rng, 6), position), (blocks,), jnp.float32, smallest / len(cuts), top_value / len(cuts))
        loudness = loudness * jnp.repeat(jnp.exp(steps), dims[position] // blocks).reshape((-1,) + (1,) * (len(dims) - 1 - position))
    return loudness


def scatter_about(own_key, dims, spread, most, cuts=(), kind=jnp.bfloat16):
    factor_of = block_levels(own_key, dims, cuts, -0.22, 0.18) if cuts else 1.0
    values = jax.random.normal(own_key, dims, jnp.float32) * spread * factor_of
    return jnp.minimum(jnp.maximum(values, -most), most).astype(kind)


def setup_inputs(seed: int = 0) -> dict:
    arg_keys = jax.random.split(jax.random.key(seed), 7)
    feats = scatter_about(arg_keys[0], (BATCH, C, G, ATOMS), 1.0, 6.0, ((0, 2), (1, 8), (3, 32)))
    neighbors = draw_neighbors(jax.random.fold_in(arg_keys[6], 71), 0)
    counts = draw_counts(jax.random.fold_in(arg_keys[6], 71), 0)
    radial = jnp.clip(2.0 + 4.0 * jax.random.uniform(arg_keys[3], (BATCH, K, EDGES), jnp.float32) ** block_levels(arg_keys[3], (BATCH, K, EDGES), ((0, 2), (2, 32)), -0.2, 0.2), 2.0, 6.0).astype(jnp.bfloat16)
    filter_weight = scatter_about(arg_keys[4], (K, C, G), 0.02, 0.3125, ((1, 8),))
    message_grad = scatter_about(arg_keys[5], (BATCH, C, G, EDGES), 0.15, 2.0, ((0, 2), (1, 8), (3, 32)))
    return {"feats": feats, "neighbors": neighbors, "counts": counts, "radial": radial, "filter_weight": filter_weight, "message_grad": message_grad}


def basis_table():
    points = jnp.arange(POINTS, dtype=jnp.float32) * jnp.float32(2.0 * 3.141592653589793 / POINTS)
    degree_index = jnp.arange(BASIS, dtype=jnp.int32)
    frequency = ((degree_index + 1) // 2).astype(jnp.float32)
    angles = frequency[:, None] * points[None, :]
    root_two = jnp.sqrt(jnp.float32(2.0))
    single = jnp.where(degree_index[:, None] == 0, jnp.ones_like(angles), jnp.where(degree_index[:, None] % 2 == 1, root_two * jnp.cos(angles), root_two * jnp.sin(angles)))
    product = single[:, None, :, None] * single[None, :, None, :]
    return product.reshape(G, SAMPLES).astype(jnp.bfloat16)

def channel_terms(gathered, grad_c, weight_c, radial_e, valid_mask, synth_table, synth_rows):
    filter_edge = jnp.dot(weight_c.T, radial_e, preferred_element_type=jnp.float32).astype(jnp.bfloat16)
    feat_grid = jnp.dot(synth_rows, gathered, preferred_element_type=jnp.float32)
    filt_grid = jnp.dot(synth_rows, filter_edge, preferred_element_type=jnp.float32)
    weighted = jnp.dot(synth_rows, grad_c, preferred_element_type=jnp.float32) * (valid_mask / SAMPLES)[None, :]
    feat_side = (weighted * filt_grid).astype(jnp.bfloat16)
    filt_side = (weighted * feat_grid).astype(jnp.bfloat16)
    edge_grad = jnp.dot(synth_table, feat_side, preferred_element_type=jnp.float32).astype(jnp.bfloat16)
    filt_grad = jnp.dot(synth_table, filt_side, preferred_element_type=jnp.float32).astype(jnp.bfloat16)
    radial_part = jnp.dot(weight_c, filt_grad, preferred_element_type=jnp.float32)
    weight_part = jnp.dot(radial_e, filt_grad.T, preferred_element_type=jnp.float32)
    return (edge_grad, radial_part, weight_part)

def reference(feats, neighbors, counts, radial, filter_weight, message_grad):
    synth_table = basis_table()
    synth_rows = synth_table.T
    feat_list = []
    radial_list = []
    weight_total = jnp.zeros((C, K, G), jnp.float32)
    for batch_row in range(BATCH):
        sources = neighbors[batch_row].reshape(-1).astype(jnp.int32)
        valid_mask = (jnp.arange(SLOTS, dtype=jnp.int32)[None, :] < counts[batch_row][:, None]).reshape(-1).astype(jnp.float32)
        radial_e = radial[batch_row]

        def per_channel(channel):
            gathered = jnp.take(feats[batch_row, channel], sources, axis=1)
            weight_c = filter_weight[:, channel, :]
            edge_grad, radial_part, weight_part = channel_terms(gathered, message_grad[batch_row, channel], weight_c, radial_e, valid_mask, synth_table, synth_rows)
            source_grad = jax.ops.segment_sum(edge_grad.astype(jnp.float32).T, sources, num_segments=ATOMS).T
            return (source_grad, radial_part, weight_part)
        source_grad, radial_part, weight_part = lax.map(per_channel, jnp.arange(C, dtype=jnp.int32))
        feat_list.append(source_grad)
        radial_list.append(lax.optimization_barrier(jnp.sum(radial_part, axis=0)))
        weight_total = weight_total + weight_part
    weight_grad = jnp.transpose(weight_total, (1, 0, 2)) / (ATOMS * BATCH)
    return (jnp.stack(feat_list), jnp.stack(radial_list), weight_grad)
```

```python
import functools

import jax
import jax.numpy as jnp
import numpy as np
from jax import lax
from jax.experimental import pallas as pl
from jax.experimental.pallas import tpu as pltpu
from jax.sharding import PartitionSpec as P

BASIS = 9
POINTS = 16
SLOTS = 32
REACH = 2
BLOCKS = 2 * REACH + 1
G = 81
SAMPLES = 256
WINDOW = 128

VMEM = pl.BlockSpec(memory_space=pltpu.VMEM)


def passed_along(value, axis, steps):
    count = lax.axis_size(axis)
    pairs = [(source, (source + steps) % count) for source in range(count)]
    return lax.ppermute(value, axis, pairs)


def basis_table():
    points = np.arange(POINTS) * (2.0 * np.pi / POINTS)
    rows = [np.ones(POINTS)]
    for k in range(1, BASIS // 2 + 1):
        rows.append(np.sqrt(2.0) * np.cos(k * points))
        rows.append(np.sqrt(2.0) * np.sin(k * points))
    single = np.stack(rows).astype(np.float32)
    product = single[:, None, :, None] * single[None, :, None, :]
    return product.reshape(G, SAMPLES).astype(jnp.bfloat16)


def dot(a, b):
    return jnp.dot(a, b, preferred_element_type=jnp.float32)


def dot_nt(a, b):
    return lax.dot_general(a, b, (((1,), (1,)), ((), ())), preferred_element_type=jnp.float32)


def selector(neighbors_ref, counts_ref, block_len, edges):
    position = lax.axis_index("atom")
    atom_count = lax.axis_size("atom")
    sources = neighbors_ref[...]
    block = lax.rem(
        lax.div(sources, block_len) - position + (REACH + atom_count), jnp.int32(atom_count)
    )
    slot = (block * block_len + lax.rem(sources, block_len)).astype(jnp.bfloat16)
    edge = lax.broadcasted_iota(jnp.int32, (SLOTS, edges), 1)
    spread = (edge % SLOTS == lax.broadcasted_iota(jnp.int32, (SLOTS, edges), 0)).astype(jnp.bfloat16)
    edge = lax.broadcasted_iota(jnp.int32, (block_len, edges), 1)
    mine = edge // SLOTS == lax.broadcasted_iota(jnp.int32, (block_len, edges), 0)
    slot_row = jnp.sum(jnp.where(mine, dot(slot, spread), 0.0), axis=0, keepdims=True)
    counts = jnp.broadcast_to(counts_ref[...], (8, block_len)).astype(jnp.bfloat16)
    count_row = dot(counts, mine.astype(jnp.bfloat16))[:1]
    in_row = (lax.broadcasted_iota(jnp.int32, (1, edges), 1) % SLOTS).astype(jnp.float32)
    slot_row = jnp.where(in_row < count_row, slot_row, -1.0)
    window = lax.broadcasted_iota(jnp.int32, (WINDOW, edges), 0).astype(jnp.float32)
    return (window == slot_row).astype(jnp.bfloat16)


def split(value, axis):
    high = value.astype(jnp.bfloat16)
    low = (value - high.astype(jnp.float32)).astype(jnp.bfloat16)
    half = value.shape[axis] // 2
    first = lax.broadcasted_iota(jnp.int32, value.shape, axis) < half
    return jnp.where(first, high.astype(jnp.float32), low.astype(jnp.float32)).astype(jnp.bfloat16)


def filter_side(
    grad_ref, weight_ref, neighbors_ref, counts_ref, radial_ref, table_ref, rows_ref,
    *refs,
):
    blocks = refs[:BLOCKS]
    weight_out, radial_out = refs[BLOCKS : BLOCKS + 2]
    sel_ref, window_ref, total_ref, moments_ref = refs[BLOCKS + 2 :]
    chan_count, _, edges = grad_ref.shape
    block_len = blocks[0].shape[1]
    sel_ref[...] = selector(neighbors_ref, counts_ref, block_len, edges)
    window_ref[...] = jnp.zeros_like(window_ref)
    total_ref[...] = jnp.zeros_like(total_ref)

    @pl.loop(0, chan_count)
    def _(c):
        for j in range(BLOCKS):
            window_ref[j * block_len : (j + 1) * block_len, :] = blocks[j][c]
        window_grid = dot_nt(rows_ref[...], window_ref[...]).astype(jnp.bfloat16)
        weighted = dot(rows_ref[...], grad_ref[c])
        feat_grid = dot(window_grid, sel_ref[...])
        filt_side = (weighted * feat_grid).astype(jnp.bfloat16)
        weight_grid = split(dot(weight_ref[c], table_ref[...]), 0)
        total_ref[...] += dot(weight_grid, filt_side)
        moments_ref[c] = dot_nt(radial_ref[...], filt_side)

    degrees = radial_ref.shape[0]
    radial_sum = (total_ref[:degrees] + total_ref[degrees:]) * (1.0 / SAMPLES)
    for j in range(radial_out.shape[0]):
        radial_out[j] = radial_sum
    moments = moments_ref[...].reshape(chan_count * degrees, SAMPLES)
    high = moments.astype(jnp.bfloat16)
    low = (moments - high.astype(jnp.float32)).astype(jnp.bfloat16)
    weight = dot_nt(high, table_ref[...]) + dot_nt(low, table_ref[...])
    weight_out[...] = weight * (1.0 / SAMPLES)


def feature_side(
    grad_ref, weight_ref, neighbors_ref, counts_ref, radial_ref, table_ref, rows_ref,
    *refs,
):
    outs = refs[:BLOCKS]
    sel_ref = refs[BLOCKS]
    chan_count, _, edges = grad_ref.shape
    block_len = outs[0].shape[1]
    sel_ref[...] = selector(neighbors_ref, counts_ref, block_len, edges)
    radial = jnp.concatenate([radial_ref[...]] * 2, axis=0)

    @pl.loop(0, chan_count)
    def _(c):
        weight_grid = split(dot_nt(rows_ref[...], weight_ref[c]), 1)
        filt_grid = dot(weight_grid, radial)
        weighted = dot(rows_ref[...], grad_ref[c])
        feat_side = (weighted * filt_grid).astype(jnp.bfloat16)
        window_grid = dot_nt(sel_ref[...], feat_side).astype(jnp.bfloat16)
        window_grad = dot(window_grid, rows_ref[...]) * (1.0 / SAMPLES)
        for j in range(BLOCKS):
            outs[j][c] = window_grad[j * block_len : (j + 1) * block_len, :]


def local(feats, neighbors, counts, radial, filter_weight, message_grad):
    table = basis_table()
    rows = jnp.asarray(np.ascontiguousarray(table.T))
    table = jnp.asarray(table)
    atom_count = lax.axis_size("atom")
    chan_devices = lax.axis_size("chan")
    _, chan_count, _, block_len = feats.shape
    degrees, edges = radial.shape[1:]
    own_block = jnp.transpose(feats[0], (0, 2, 1))
    halo = [
        own_block if offset == 0 else passed_along(own_block, "atom", -offset)
        for offset in range(-REACH, REACH + 1)
    ]
    weight = jnp.transpose(filter_weight, (1, 0, 2))
    weight = jnp.concatenate([weight, weight], axis=1)
    common = (message_grad[0], weight, neighbors[0], counts, radial[0], table, rows)
    weight_part, radial_part = pl.pallas_call(
        filter_side,
        out_shape=(
            jax.ShapeDtypeStruct((chan_count * degrees, G), jnp.float32),
            jax.ShapeDtypeStruct((chan_devices, degrees, edges), jnp.float32),
        ),
        in_specs=[VMEM] * (len(common) + BLOCKS),
        out_specs=(VMEM, VMEM),
        scratch_shapes=[
            pltpu.VMEM((WINDOW, edges), jnp.bfloat16),
            pltpu.VMEM((WINDOW, G), jnp.bfloat16),
            pltpu.VMEM((2 * degrees, edges), jnp.float32),
            pltpu.VMEM((chan_count, degrees, SAMPLES), jnp.float32),
        ],
        cost_estimate=pl.CostEstimate(flops=6 * 10**9, bytes_accessed=4 * 10**6, transcendentals=0),
        name="filter_side",
    )(*common, *halo)

    group = ("atom", "rep")
    members = lax.axis_size(group)
    pieces = lax.all_to_all(weight_part.reshape(members, -1, G), group, 0, 0, tiled=True)
    radial_parts = lax.all_to_all(radial_part, "chan", 0, 0, tiled=True)

    window_grads = pl.pallas_call(
        feature_side,
        out_shape=[jax.ShapeDtypeStruct((chan_count, block_len, G), jnp.float32)] * BLOCKS,
        in_specs=[VMEM] * len(common),
        out_specs=[VMEM] * BLOCKS,
        scratch_shapes=[pltpu.VMEM((WINDOW, edges), jnp.bfloat16)],
        cost_estimate=pl.CostEstimate(flops=6 * 10**9, bytes_accessed=4 * 10**6, transcendentals=0),
        name="feature_side",
    )(*common)

    piece = jnp.sum(pieces, axis=0, keepdims=True) / (atom_count * block_len * lax.axis_size("rep"))
    weight_grad = lax.all_to_all(jnp.broadcast_to(piece, pieces.shape), group, 0, 0, tiled=True)
    weight_grad = jnp.transpose(weight_grad.reshape(chan_count, degrees, G), (1, 0, 2))
    feat_grad = window_grads[REACH]
    for offset in range(-REACH, REACH + 1):
        if offset != 0:
            feat_grad = feat_grad + passed_along(window_grads[offset + REACH], "atom", offset)
    feat_grad = jnp.transpose(feat_grad, (0, 2, 1))[None]
    radial_grad = jnp.sum(radial_parts, axis=0, keepdims=True)
    return (feat_grad, radial_grad, weight_grad)


def solution(mesh):
    placed = (
        P("rep", "chan", None, "atom"),
        P("rep", "atom", None),
        P("rep", "atom"),
        P("rep", None, "atom"),
        P(None, "chan", None),
        P("rep", "chan", None, "atom"),
    )
    return jax.shard_map(
        local,
        mesh=mesh,
        in_specs=placed,
        out_specs=(P("rep", "chan", None, "atom"), P("rep", None, "atom"), P(None, "chan", None)),
        check_vma=False,
    )
```

```python
import jax
import jax.numpy as jnp
import numpy as np
from jax import lax
from jax.experimental import pallas as pl
from jax.experimental.pallas import tpu as pltpu
from jax.sharding import PartitionSpec as P


BASIS = 9
POINTS = 16
SLOTS = 32
REACH = 2
G = 81
SAMPLES = 256
WINDOW = 80
LANES = 128
UNROLL = 4
VMEM_BYTES = 24 * 2**20

VMEM = pl.BlockSpec(memory_space=pltpu.VMEM)


def passed_along(value, axis, steps):
    count = lax.axis_size(axis)
    pairs = [(source, (source + steps) % count) for source in range(count)]
    return lax.ppermute(value, axis, pairs)


def exchanged(value, axis, bit):
    return lax.ppermute(value, axis, [(i, i ^ bit) for i in range(lax.axis_size(axis))])


def basis_table():
    points = np.arange(POINTS) * (2.0 * np.pi / POINTS)
    rows = [np.ones(POINTS)]
    for k in range(1, BASIS // 2 + 1):
        rows.append(np.sqrt(2.0) * np.cos(k * points))
        rows.append(np.sqrt(2.0) * np.sin(k * points))
    single = np.stack(rows).astype(np.float32)
    product = single[:, None, :, None] * single[None, :, None, :]
    return product.reshape(G, SAMPLES).astype(jnp.bfloat16)


def dot(a, b):
    return jnp.dot(a, b, preferred_element_type=jnp.float32)


def dot_nt(a, b):
    return lax.dot_general(a, b, (((1,), (1,)), ((), ())), preferred_element_type=jnp.float32)


def selector(neighbors_ref, counts_ref, block_len, edges):
    position = lax.axis_index("atom")
    atom_count = lax.axis_size("atom")
    sources = neighbors_ref[...]
    block = lax.rem(
        lax.div(sources, block_len) - position + (REACH + atom_count), jnp.int32(atom_count)
    )
    half = lax.div(block, jnp.int32(2))
    block = jnp.where(lax.rem(block, jnp.int32(2)) == 1, half + (REACH + 1), half)
    slot = (block * block_len + lax.rem(sources, block_len)).astype(jnp.bfloat16)
    edge = lax.broadcasted_iota(jnp.int32, (SLOTS, edges), 1)
    spread = (edge % SLOTS == lax.broadcasted_iota(jnp.int32, (SLOTS, edges), 0)).astype(jnp.bfloat16)
    edge = lax.broadcasted_iota(jnp.int32, (block_len, edges), 1)
    mine = edge // SLOTS == lax.broadcasted_iota(jnp.int32, (block_len, edges), 0)
    slot_row = jnp.sum(jnp.where(mine, dot(slot, spread), 0.0), axis=0, keepdims=True)
    counts = jnp.broadcast_to(counts_ref[...], (8, block_len)).astype(jnp.bfloat16)
    count_row = dot(counts, mine.astype(jnp.bfloat16))[:1]
    in_row = (lax.broadcasted_iota(jnp.int32, (1, edges), 1) % SLOTS).astype(jnp.float32)
    slot_row = jnp.where(in_row < count_row, slot_row, -1.0)
    window = lax.broadcasted_iota(jnp.int32, (WINDOW, edges), 0).astype(jnp.float32)
    return (window == slot_row).astype(jnp.bfloat16)


def split(value):
    high = value.astype(jnp.bfloat16)
    return high, (value - high.astype(jnp.float32)).astype(jnp.bfloat16)


def filter_grids(weight_ref, table_ref, grids_ref):
    for half, value in enumerate(split(dot(weight_ref[...], table_ref[...]))):
        for run in range(SAMPLES // LANES):
            part = value[:, run * LANES : (run + 1) * LANES]
            grids_ref[half, run] = part.astype(jnp.float32)


def filter_grid(grids_ref, c, degrees, chan_count):
    rows = pl.ds(c, degrees, stride=chan_count)
    halves = [
        jnp.concatenate([grids_ref[half, run, rows, :] for run in range(SAMPLES // LANES)], axis=1)
        for half in range(2)
    ]
    return jnp.concatenate(halves, axis=0)


def edge_terms(
    edge_grad_ref, weight_ref, neighbors_ref, counts_ref, radial_ref, table_ref, rows_ref,
    even_ref, odd_ref,
    weight_out, radial_out, left_out, own_out, right_out, odd_out,
    grad_ref, sel_ref, grids_ref, window_ref, moments_ref,
):
    grad_ref[...] = jnp.swapaxes(edge_grad_ref[...], 0, 1)
    chan_count, _, edges = grad_ref.shape
    degrees = radial_ref.shape[0]
    even_len = even_ref.shape[1]
    block_len = own_out.shape[1]
    sel_ref[...] = selector(neighbors_ref, counts_ref, block_len, edges)
    filter_grids(weight_ref, table_ref, grids_ref)
    window_ref[:, :even_len, :] = even_ref[...]
    first = pl.multiple_of(lax.rem(lax.axis_index("atom"), 2) * block_len, block_len)
    window_ref[:, even_len:, :] = odd_ref[:, pl.ds(first, REACH * block_len), :]
    radial = jnp.concatenate([radial_ref[...]] * 2, axis=0)

    def channel(c, total):
        weighted = dot(rows_ref[...], grad_ref[c])
        weight_grid = filter_grid(grids_ref, c, degrees, chan_count)
        filt_grid = dot(weight_grid.T.astype(jnp.bfloat16), radial)
        window_grid = dot(window_ref[c], table_ref[...]).T.astype(jnp.bfloat16)
        feat_grid = dot(window_grid, sel_ref[...])
        feat_side = (weighted * filt_grid).astype(jnp.bfloat16)
        filt_side = (weighted * feat_grid).astype(jnp.bfloat16)
        moments_ref[:, c, :] = dot_nt(radial_ref[...], filt_side)
        total = total + dot(weight_grid.astype(jnp.bfloat16), filt_side)
        window_sum = dot_nt(sel_ref[...], feat_side).astype(jnp.bfloat16)
        window_grad = dot(window_sum, rows_ref[...]) * (1.0 / SAMPLES)
        for j, out in enumerate((left_out, own_out, right_out)):
            out[c] = window_grad[j * block_len : (j + 1) * block_len, :]
        odd_out[c] = window_grad[even_len:, :]
        return total

    total = lax.fori_loop(
        0, chan_count, channel, jnp.zeros((2 * degrees, edges), jnp.float32), unroll=UNROLL
    )
    radial_sum = (total[:degrees] + total[degrees:]) * (1.0 / SAMPLES)
    for j in range(radial_out.shape[0]):
        radial_out[j] = radial_sum
    high, low = split(moments_ref[...].reshape(degrees * chan_count, SAMPLES))
    weight = dot_nt(high, table_ref[...]) + dot_nt(low, table_ref[...])
    weight_out[...] = weight * (1.0 / SAMPLES)


def stack_blocks(left_ref, own_ref, right_ref, out_ref):
    block_len = own_ref.shape[1]
    for j, ref in enumerate((left_ref, own_ref, right_ref)):
        out_ref[:, j * block_len : (j + 1) * block_len, :] = ref[...]


def pair_sums(left_ref, own_ref, right_ref, odd_ref, left_out, own_out, right_out):
    block_len = own_ref.shape[1]
    second = lax.rem(lax.axis_index("atom"), 2) == 1
    before, after = odd_ref[:, :block_len, :], odd_ref[:, block_len:, :]
    zero = jnp.zeros_like(before)
    left_out[...] = (left_ref[...] + jnp.where(second, before, zero)).astype(left_out.dtype)
    right_out[...] = (right_ref[...] + jnp.where(second, zero, after)).astype(right_out.dtype)
    own_out[...] = own_ref[...] + jnp.where(second, after, before)


def local(feats, neighbors, counts, radial, filter_weight, message_grad):
    table = basis_table()
    rows = jnp.asarray(np.ascontiguousarray(table.T))
    table = jnp.asarray(table)
    atom_count = lax.axis_size("atom")
    chan_devices = lax.axis_size("chan")
    _, chan_count, _, block_len = feats.shape
    degrees, edges = radial.shape[1:]
    params = pltpu.CompilerParams(vmem_limit_bytes=VMEM_BYTES)

    own_block = jnp.transpose(feats[0], (0, 2, 1))
    left = passed_along(own_block, "atom", REACH)
    right = passed_along(own_block, "atom", -REACH)
    even = pl.pallas_call(
        stack_blocks,
        out_shape=jax.ShapeDtypeStruct((chan_count, (REACH + 1) * block_len, G), feats.dtype),
        in_specs=[VMEM] * 3,
        out_specs=VMEM,
        compiler_params=params,
        cost_estimate=pl.CostEstimate(flops=10**9, bytes_accessed=6 * 10**7, transcendentals=0),
        name="stack_blocks",
    )(left, own_block, right)
    odd = exchanged(even, "atom", 1)

    weight = filter_weight.reshape(degrees * chan_count, G)
    block = jax.ShapeDtypeStruct((chan_count, block_len, G), jnp.float32)
    weight_part, radial_part, left, own, right, odd = pl.pallas_call(
        edge_terms,
        out_shape=(
            jax.ShapeDtypeStruct((degrees * chan_count, G), jnp.float32),
            jax.ShapeDtypeStruct((chan_devices, degrees, edges), jnp.float32),
            block,
            block,
            block,
            jax.ShapeDtypeStruct((chan_count, REACH * block_len, G), jnp.float32),
        ),
        in_specs=[VMEM] * 9,
        out_specs=(VMEM,) * 6,
        scratch_shapes=[
            pltpu.VMEM((chan_count, G, edges), jnp.bfloat16),
            pltpu.VMEM((WINDOW, edges), jnp.bfloat16),
            pltpu.VMEM((2, SAMPLES // LANES, degrees * chan_count, LANES), jnp.float32),
            pltpu.VMEM((chan_count, WINDOW, G), jnp.bfloat16),
            pltpu.VMEM((degrees, chan_count, SAMPLES), jnp.float32),
        ],
        compiler_params=params,
        cost_estimate=pl.CostEstimate(flops=10**10, bytes_accessed=4 * 10**6, transcendentals=0),
        name="edge_terms",
    )(jnp.swapaxes(message_grad[0], 0, 1), weight, neighbors[0], counts, radial[0], table, rows, even, odd)

    group = ("atom", "rep")
    members = lax.axis_size(group)
    pieces = lax.all_to_all(weight_part.reshape(members, -1, G), group, 0, 0, tiled=True)
    piece = jnp.sum(pieces, axis=0, keepdims=True) / (atom_count * block_len * lax.axis_size("rep"))
    weight_grad = lax.all_to_all(
        jnp.broadcast_to(piece, pieces.shape), group, 0, 0, tiled=True
    )
    weight_grad = weight_grad.reshape(degrees, chan_count, G)
    radial_parts = lax.all_to_all(radial_part, "chan", 0, 0, tiled=True)
    radial_grad = jnp.sum(radial_parts, axis=0, keepdims=True)

    odd = exchanged(odd, "atom", 1)
    sent = jax.ShapeDtypeStruct(block.shape, jnp.bfloat16)
    left, own, right = pl.pallas_call(
        pair_sums,
        out_shape=[sent, block, sent],
        in_specs=[VMEM] * 4,
        out_specs=[VMEM] * 3,
        compiler_params=params,
        cost_estimate=pl.CostEstimate(flops=10**6, bytes_accessed=10**6, transcendentals=0),
        name="pair_sums",
    )(left, own, right, odd)
    left = passed_along(left, "atom", -REACH)
    right = passed_along(right, "atom", REACH)
    feat_grad = own + left.astype(jnp.float32) + right.astype(jnp.float32)
    feat_grad = jnp.transpose(feat_grad, (0, 2, 1))[None]
    return (feat_grad, radial_grad, weight_grad)


def solution(mesh):
    placed = (
        P("rep", "chan", None, "atom"),
        P("rep", "atom", None),
        P("rep", "atom"),
        P("rep", None, "atom"),
        P(None, "chan", None),
        P("rep", "chan", None, "atom"),
    )

    return jax.shard_map(
        local,
        mesh=mesh,
        in_specs=placed,
        out_specs=(P("rep", "chan", None, "atom"), P("rep", None, "atom"), P(None, "chan", None)),
        check_vma=False,
    )
```

```python
import jax
import jax.numpy as jnp
import numpy as np
from jax import lax
from jax.experimental import pallas as pl
from jax.experimental.pallas import tpu as pltpu
from jax.sharding import PartitionSpec as P


BASIS = 9
POINTS = 16
SLOTS = 32
REACH = 2
G = 81
SAMPLES = 256
WINDOW = 80
LANES = 128
UNROLL = 8
VMEM_BYTES = 24 * 2**20

VMEM = pl.BlockSpec(memory_space=pltpu.VMEM)


def passed_along(value, axis, steps):
    count = lax.axis_size(axis)
    pairs = [(source, (source + steps) % count) for source in range(count)]
    return lax.ppermute(value, axis, pairs)


def exchanged(value, axis, bit):
    return lax.ppermute(value, axis, [(i, i ^ bit) for i in range(lax.axis_size(axis))])


def basis_table():
    points = np.arange(POINTS) * (2.0 * np.pi / POINTS)
    rows = [np.ones(POINTS)]
    for k in range(1, BASIS // 2 + 1):
        rows.append(np.sqrt(2.0) * np.cos(k * points))
        rows.append(np.sqrt(2.0) * np.sin(k * points))
    single = np.stack(rows).astype(np.float32)
    product = single[:, None, :, None] * single[None, :, None, :]
    return product.reshape(G, SAMPLES).astype(jnp.bfloat16)


def dot(a, b):
    return jnp.dot(a, b, preferred_element_type=jnp.float32)


def dot_nt(a, b):
    return lax.dot_general(a, b, (((1,), (1,)), ((), ())), preferred_element_type=jnp.float32)


def selector(neighbors_ref, counts_ref, block_len, edges):
    position = lax.axis_index("atom")
    atom_count = lax.axis_size("atom")
    sources = neighbors_ref[...]
    block = lax.rem(
        lax.div(sources, block_len) - position + (REACH + atom_count), jnp.int32(atom_count)
    )
    half = lax.div(block, jnp.int32(2))
    block = jnp.where(lax.rem(block, jnp.int32(2)) == 1, half + (REACH + 1), half)
    slot = (block * block_len + lax.rem(sources, block_len)).astype(jnp.bfloat16)
    edge = lax.broadcasted_iota(jnp.int32, (SLOTS, edges), 1)
    spread = (edge % SLOTS == lax.broadcasted_iota(jnp.int32, (SLOTS, edges), 0)).astype(jnp.bfloat16)
    edge = lax.broadcasted_iota(jnp.int32, (block_len, edges), 1)
    mine = edge // SLOTS == lax.broadcasted_iota(jnp.int32, (block_len, edges), 0)
    slot_row = jnp.sum(jnp.where(mine, dot(slot, spread), 0.0), axis=0, keepdims=True)
    counts = jnp.broadcast_to(counts_ref[...], (8, block_len)).astype(jnp.bfloat16)
    count_row = dot(counts, mine.astype(jnp.bfloat16))[:1]
    in_row = (lax.broadcasted_iota(jnp.int32, (1, edges), 1) % SLOTS).astype(jnp.float32)
    slot_row = jnp.where(in_row < count_row, slot_row, -1.0)
    window = lax.broadcasted_iota(jnp.int32, (WINDOW, edges), 0).astype(jnp.float32)
    return (window == slot_row).astype(jnp.bfloat16)


def split(value):
    high = value.astype(jnp.bfloat16)
    return high, (value - high.astype(jnp.float32)).astype(jnp.bfloat16)


def filter_grids(weight_ref, table_ref, grids_ref):
    for half, value in enumerate(split(dot(weight_ref[...], table_ref[...]))):
        for run in range(SAMPLES // LANES):
            part = value[:, run * LANES : (run + 1) * LANES]
            grids_ref[half, run] = part.astype(jnp.float32)


def filter_grid(grids_ref, c, degrees, chan_count):
    rows = pl.ds(c, degrees, stride=chan_count)
    halves = [
        jnp.concatenate([grids_ref[half, run, rows, :] for run in range(SAMPLES // LANES)], axis=1)
        for half in range(2)
    ]
    return jnp.concatenate(halves, axis=0)


def edge_terms(
    edge_grad_ref, weight_ref, neighbors_ref, counts_ref, radial_ref, table_ref, rows_ref,
    even_ref, odd_ref,
    weight_out, radial_out, left_out, own_out, right_out, odd_out,
    grad_ref, sel_ref, grids_ref, window_ref, moments_ref,
):
    grad_ref[...] = jnp.swapaxes(edge_grad_ref[...], 0, 1)
    chan_count, _, edges = grad_ref.shape
    degrees = radial_ref.shape[0]
    even_len = even_ref.shape[1]
    block_len = own_out.shape[1]
    sel_ref[...] = selector(neighbors_ref, counts_ref, block_len, edges)
    filter_grids(weight_ref, table_ref, grids_ref)
    window_ref[:, :even_len, :] = even_ref[...]
    first = pl.multiple_of(lax.rem(lax.axis_index("atom"), 2) * block_len, block_len)
    window_ref[:, even_len:, :] = odd_ref[:, pl.ds(first, REACH * block_len), :]
    radial = jnp.concatenate([radial_ref[...]] * 2, axis=0)

    def channel(c, total):
        weighted = dot(rows_ref[...], grad_ref[c])
        weight_grid = filter_grid(grids_ref, c, degrees, chan_count)
        filt_grid = dot(weight_grid.T.astype(jnp.bfloat16), radial)
        window_grid = dot(window_ref[c], table_ref[...]).T.astype(jnp.bfloat16)
        feat_grid = dot(window_grid, sel_ref[...])
        feat_side = (weighted * filt_grid).astype(jnp.bfloat16)
        filt_side = (weighted * feat_grid).astype(jnp.bfloat16)
        moments_ref[:, c, :] = dot_nt(radial_ref[...], filt_side)
        total = total + dot(weight_grid.astype(jnp.bfloat16), filt_side)
        window_sum = dot_nt(sel_ref[...], feat_side).astype(jnp.bfloat16)
        window_grad = dot(window_sum, rows_ref[...]) * (1.0 / SAMPLES)
        for j, out in enumerate((left_out, own_out, right_out)):
            out[c] = window_grad[j * block_len : (j + 1) * block_len, :]
        odd_out[c] = window_grad[even_len:, :]
        return total

    total = lax.fori_loop(
        0, chan_count, channel, jnp.zeros((2 * degrees, edges), jnp.float32), unroll=UNROLL
    )
    radial_sum = (total[:degrees] + total[degrees:]) * (1.0 / SAMPLES)
    radial_sum = radial_sum.astype(radial_out.dtype)
    for j in range(radial_out.shape[0]):
        radial_out[j] = radial_sum
    high, low = split(moments_ref[...].reshape(degrees * chan_count, SAMPLES))
    weight = dot_nt(high, table_ref[...]) + dot_nt(low, table_ref[...])
    weight_out[...] = weight * (1.0 / SAMPLES)


def copy_block(block_ref, out_ref):
    out_ref[...] = block_ref[...]


def join_pieces(pieces_ref, out_ref):
    count, length, _ = pieces_ref.shape
    for i in range(count):
        out_ref[i * length : (i + 1) * length, :] = pieces_ref[i]


def stack_blocks(left_ref, own_ref, right_ref, out_ref):
    block_len = own_ref.shape[1]
    for j, ref in enumerate((left_ref, own_ref, right_ref)):
        out_ref[:, j * block_len : (j + 1) * block_len, :] = ref[...]


def pair_sums(left_ref, own_ref, right_ref, odd_ref, left_out, own_out, right_out):
    block_len = own_ref.shape[1]
    second = lax.rem(lax.axis_index("atom"), 2) == 1
    before, after = odd_ref[:, :block_len, :], odd_ref[:, block_len:, :]
    zero = jnp.zeros_like(before)
    left_out[...] = (left_ref[...] + jnp.where(second, before, zero)).astype(left_out.dtype)
    right_out[...] = (right_ref[...] + jnp.where(second, zero, after)).astype(right_out.dtype)
    own_out[...] = own_ref[...] + jnp.where(second, after, before)


def local(feats, neighbors, counts, radial, filter_weight, message_grad):
    table = basis_table()
    rows = jnp.asarray(np.ascontiguousarray(table.T))
    table = jnp.asarray(table)
    atom_count = lax.axis_size("atom")
    chan_devices = lax.axis_size("chan")
    _, chan_count, _, block_len = feats.shape
    degrees, edges = radial.shape[1:]
    params = pltpu.CompilerParams(vmem_limit_bytes=VMEM_BYTES)

    own_block = jnp.transpose(feats[0], (0, 2, 1))
    left = passed_along(own_block, "atom", REACH)
    right = passed_along(own_block, "atom", -REACH)
    own = pl.pallas_call(
        copy_block,
        out_shape=jax.ShapeDtypeStruct(own_block.shape, own_block.dtype),
        in_specs=[VMEM],
        out_specs=VMEM,
        compiler_params=params,
        cost_estimate=pl.CostEstimate(flops=10**6, bytes_accessed=10**6, transcendentals=0),
        name="copy_block",
    )(own_block)
    even = pl.pallas_call(
        stack_blocks,
        out_shape=jax.ShapeDtypeStruct((chan_count, (REACH + 1) * block_len, G), feats.dtype),
        in_specs=[VMEM] * 3,
        out_specs=VMEM,
        compiler_params=params,
        cost_estimate=pl.CostEstimate(flops=10**9, bytes_accessed=6 * 10**7, transcendentals=0),
        name="stack_blocks",
    )(left, own, right)
    odd = exchanged(even, "atom", 1)

    weight = filter_weight.reshape(degrees * chan_count, G)
    block = jax.ShapeDtypeStruct((chan_count, block_len, G), jnp.float32)
    weight_part, radial_part, left, own, right, odd = pl.pallas_call(
        edge_terms,
        out_shape=(
            jax.ShapeDtypeStruct((degrees * chan_count, G), jnp.float32),
            jax.ShapeDtypeStruct((chan_devices, degrees, edges), jnp.bfloat16),
            block,
            block,
            block,
            jax.ShapeDtypeStruct((chan_count, REACH * block_len, G), jnp.float32),
        ),
        in_specs=[VMEM] * 9,
        out_specs=(VMEM,) * 6,
        scratch_shapes=[
            pltpu.VMEM((chan_count, G, edges), jnp.bfloat16),
            pltpu.VMEM((WINDOW, edges), jnp.bfloat16),
            pltpu.VMEM((2, SAMPLES // LANES, degrees * chan_count, LANES), jnp.float32),
            pltpu.VMEM((chan_count, WINDOW, G), jnp.bfloat16),
            pltpu.VMEM((degrees, chan_count, SAMPLES), jnp.float32),
        ],
        compiler_params=params,
        cost_estimate=pl.CostEstimate(flops=10**10, bytes_accessed=4 * 10**6, transcendentals=0),
        name="edge_terms",
    )(jnp.swapaxes(message_grad[0], 0, 1), weight, neighbors[0], counts, radial[0], table, rows, even, odd)

    group = ("atom", "rep")
    members = lax.axis_size(group)
    pieces = lax.all_to_all(weight_part.reshape(members, -1, G), group, 0, 0, tiled=True)
    piece = jnp.sum(pieces, axis=0, keepdims=True) / (atom_count * block_len * lax.axis_size("rep"))
    weight_grad = lax.all_to_all(
        jnp.broadcast_to(piece, pieces.shape), group, 0, 0, tiled=True
    )
    weight_grad = pl.pallas_call(
        join_pieces,
        out_shape=jax.ShapeDtypeStruct((degrees * chan_count, G), jnp.float32),
        in_specs=[VMEM],
        out_specs=VMEM,
        compiler_params=params,
        cost_estimate=pl.CostEstimate(flops=10**6, bytes_accessed=10**6, transcendentals=0),
        name="join_pieces",
    )(weight_grad).reshape(degrees, chan_count, G)
    radial_parts = lax.all_to_all(radial_part, "chan", 0, 0, tiled=True)
    radial_grad = jnp.sum(radial_parts.astype(jnp.float32), axis=0, keepdims=True)

    odd = exchanged(odd, "atom", 1)
    sent = jax.ShapeDtypeStruct(block.shape, jnp.bfloat16)
    left, own, right = pl.pallas_call(
        pair_sums,
        out_shape=[sent, block, sent],
        in_specs=[VMEM] * 4,
        out_specs=[VMEM] * 3,
        compiler_params=params,
        cost_estimate=pl.CostEstimate(flops=10**6, bytes_accessed=10**6, transcendentals=0),
        name="pair_sums",
    )(left, own, right, odd)
    left = passed_along(left, "atom", -REACH)
    right = passed_along(right, "atom", REACH)
    feat_grad = own + left.astype(jnp.float32) + right.astype(jnp.float32)
    feat_grad = jnp.transpose(feat_grad, (0, 2, 1))[None]
    return (feat_grad, radial_grad, weight_grad)


def solution(mesh):
    placed = (
        P("rep", "chan", None, "atom"),
        P("rep", "atom", None),
        P("rep", "atom"),
        P("rep", None, "atom"),
        P(None, "chan", None),
        P("rep", "chan", None, "atom"),
    )

    return jax.shard_map(
        local,
        mesh=mesh,
        in_specs=placed,
        out_specs=(P("rep", "chan", None, "atom"), P("rep", None, "atom"), P(None, "chan", None)),
        check_vma=False,
    )
```
